32 devices in a mesh: groups: 2 (over x), seq: 16 (over z, y, core).
Axes of the slice: x: 2, y: 2, z: 4, core: 2. Of those that a mesh axis runs over, the one named last changes fastest.
Arguments:
- queries: bfloat16 [4096, 2048], P(('groups', 'seq')), parts along dimension 0, may hold values from -8 to 8
- key_input: bfloat16 [4096, 2048], P(('groups', 'seq')), parts along dimension 0, may hold values from -4.5 to 4.5
- value_input: bfloat16 [4096, 2048], P(('groups', 'seq')), parts along dimension 0, may hold values from -6 to 6
- cotangent: bfloat16 [4096, 2048], P(('groups', 'seq')), parts along dimension 0, may hold values from -6 to 6
Outputs:
- attended: bfloat16 [4096, 2048], P(('groups', 'seq')), parts along dimension 0
- grad_queries: bfloat16 [4096, 2048], P(('groups', 'seq')), parts along dimension 0
- grad_keys: bfloat16 [4096, 2048], P(('groups', 'seq')), parts along dimension 0
- grad_values: bfloat16 [4096, 2048], P(('groups', 'seq')), parts along dimension 0
The draws below stay inside these ranges and needn't reach their ends.
There are 2 independent parts, one for each index of `groups`. The reference program is written for one: setup_inputs(seed, part) draws one part's arguments, and reference() takes and returns one part's arrays. A program takes and returns all parts, laid end to end along the dimension named above; each array names one. Nothing has to cross between parts.
All inputs are finite; a program needn't handle non-finite values.
Results may differ from the reference program's by a relative error of at most 0.024.
Values may be sent and summed in bfloat16 or wider, within the bound.
A program may use at most 128 MiB of HBM per device.

```python
import functools
import math
import jax
import jax.numpy as jnp
from jax import lax

HEADS = 16
HEAD_DIM = 128
BLOCK = 64
LEVELS = 3
SEQ_LEN = 2048


def paired_draw(key):
    feat_width = HEADS * HEAD_DIM
    query_key = jax.random.fold_in(key, 11)
    keys_key = jax.random.fold_in(key, 12)
    query_draw = jnp.clip(2.0 * jax.random.normal(query_key, (SEQ_LEN, feat_width), jnp.float32), -8.0, 8.0)
    keys_draw = jnp.clip(jax.random.normal(keys_key, (SEQ_LEN, feat_width), jnp.float32), -4.5, 4.5)
    return (query_draw, keys_draw)


def draw_queries(key, part):
    return paired_draw(key)[0].astype(jnp.bfloat16)


def draw_key_input(key, part):
    return paired_draw(key)[1].astype(jnp.bfloat16)


def block_scale(own_key, extent, cuts, least, high):
    level = 1.0
    for dim, shards_of in cuts:
        heights = jax.random.uniform(jax.random.fold_in(jax.random.fold_in(own_key, 6), dim), (shards_of,), jnp.float32, least / len(cuts), high / len(cuts))
        level = level * jnp.repeat(jnp.exp(heights), extent[dim] // shards_of).reshape((-1,) + (1,) * (len(extent) - 1 - dim))
    return level


def normal_values(own_key, extent, scale, limit, cuts=(), held_as=jnp.bfloat16):
    array = jax.random.normal(own_key, extent, jnp.float32) * scale
    if len(cuts) > 0:
        array = block_scale(own_key, extent, cuts, -0.22, 0.18) * array
    return jnp.clip(array, min=-limit, max=limit).astype(held_as)


def setup_inputs(seed: int = 0, part: int = 0) -> dict:
    key_of = jax.random.split(jax.random.key(seed), 5)
    part_keys = jax.random.split(jax.random.fold_in(key_of[4], part), 5)
    queries = draw_queries(jax.random.fold_in(jax.random.fold_in(key_of[4], part), 71), part)
    key_input = draw_key_input(jax.random.fold_in(jax.random.fold_in(key_of[4], part), 71), part)
    value_input = normal_values(part_keys[2], (SEQ_LEN, HEADS * HEAD_DIM), 1.0, 6.0, ((0, 16),))
    cotangent = normal_values(part_keys[3], (SEQ_LEN, HEADS * HEAD_DIM), 1.0, 6.0, ((0, 16),))
    return dict(queries=queries, key_input=key_input, value_input=value_input, cotangent=cotangent)


log_two = math.log(2.0)
masked_score = -1.0e30


def halve_rows(rows_in):
    wide = rows_in.astype(jnp.float32).reshape(rows_in.shape[0] // 2, 2, rows_in.shape[1])
    return ((wide[:, 0] + wide[:, 1]) * 0.5).astype(jnp.bfloat16)


def reference(queries, key_input, value_input, cotangent):
    feat_width = HEADS * HEAD_DIM
    scale = HEAD_DIM ** -0.5
    block_total = SEQ_LEN // BLOCK
    key_levels = [key_input]
    value_levels = [value_input]
    for height in range(1, LEVELS):
        key_levels.append(halve_rows(key_levels[-1]))
        value_levels.append(halve_rows(value_levels[-1]))
    key_padded = [jnp.pad(x, ((BLOCK, BLOCK), (0, 0))) for x in key_levels]
    value_padded = [jnp.pad(x, ((BLOCK, BLOCK), (0, 0))) for x in value_levels]
    acc_keys = [jnp.zeros(x.shape, jnp.float32) for x in key_padded]
    acc_values = [jnp.zeros(x.shape, jnp.float32) for x in value_padded]
    col_block = jnp.arange(3 * BLOCK) // BLOCK

    def advance(carry, block_no):
        acc_k, acc_v = carry
        start = (block_no * BLOCK).astype(jnp.int32)
        query_heads = lax.dynamic_slice_in_dim(queries, start, BLOCK, 0).astype(jnp.float32).reshape(BLOCK, HEADS, HEAD_DIM)
        grad_heads = lax.dynamic_slice_in_dim(cotangent, start, BLOCK, 0).astype(jnp.float32).reshape(BLOCK, HEADS, HEAD_DIM)
        score_list = []
        key_list = []
        value_list = []
        starts = []
        for height in range(LEVELS):
            coarse_no = jnp.right_shift(block_no, height)
            first_row = (coarse_no * BLOCK).astype(jnp.int32)
            key_rows = lax.dynamic_slice_in_dim(key_padded[height], first_row, 3 * BLOCK, 0).astype(jnp.float32).reshape(3 * BLOCK, HEADS, HEAD_DIM)
            value_rows = lax.dynamic_slice_in_dim(value_padded[height], first_row, 3 * BLOCK, 0).astype(jnp.float32).reshape(3 * BLOCK, HEADS, HEAD_DIM)
            scores = jnp.einsum('qhd,khd->hqk', query_heads, key_rows) * scale + height * log_two
            level_blocks = block_total >> height
            valid_mask = (col_block == 1) | ((col_block == 0) & (coarse_no >= 1)) | ((col_block == 2) & (coarse_no + 1 < level_blocks))
            scores = jnp.where(valid_mask[None, None, :], scores, masked_score)
            score_list.append(scores)
            key_list.append(key_rows)
            value_list.append(value_rows)
            starts.append(first_row)
        largest = functools.reduce(jnp.maximum, [jnp.max(s, axis=-1) for s in score_list])
        totals = functools.reduce(jnp.add, [jnp.sum(jnp.exp(s - largest[..., None]), axis=-1) for s in score_list])
        log_total = largest + jnp.log(totals)
        output = jnp.zeros((BLOCK, HEADS, HEAD_DIM), jnp.float32)
        rounded_list = []
        for height in range(LEVELS):
            weights = jnp.exp(score_list[height] - log_total[..., None])
            rounded = lax.optimization_barrier(weights.astype(jnp.bfloat16)).astype(jnp.float32)
            rounded_list.append(rounded)
            output = output + jnp.einsum('hqk,khd->qhd', rounded, value_list[height])
        attended_block = output.reshape(BLOCK, feat_width).astype(jnp.bfloat16)
        row_dots = jnp.sum(grad_heads * attended_block.astype(jnp.float32).reshape(BLOCK, HEADS, HEAD_DIM), axis=-1).T
        grad_q = jnp.zeros((BLOCK, HEADS, HEAD_DIM), jnp.float32)
        new_k = list(acc_k)
        new_v = list(acc_v)
        for height in range(LEVELS):
            weights = jnp.exp(score_list[height] - log_total[..., None])
            grad_weights = jnp.einsum('qhd,khd->hqk', grad_heads, value_list[height])
            grad_scores = lax.optimization_barrier((weights * (grad_weights - row_dots[..., None]) * scale).astype(jnp.bfloat16)).astype(jnp.float32)
            grad_q = grad_q + jnp.einsum('hqk,khd->qhd', grad_scores, key_list[height])
            key_part = jnp.einsum('hqk,qhd->khd', grad_scores, query_heads).reshape(3 * BLOCK, feat_width)
            value_part = jnp.einsum('hqk,qhd->khd', rounded_list[height], grad_heads).reshape(3 * BLOCK, feat_width)
            old_k = lax.dynamic_slice_in_dim(new_k[height], starts[height], 3 * BLOCK, 0)
            old_v = lax.dynamic_slice_in_dim(new_v[height], starts[height], 3 * BLOCK, 0)
            new_k[height] = lax.dynamic_update_slice_in_dim(new_k[height], old_k + key_part, starts[height], 0)
            new_v[height] = lax.dynamic_update_slice_in_dim(new_v[height], old_v + value_part, starts[height], 0)
        grad_block = grad_q.reshape(BLOCK, feat_width).astype(jnp.bfloat16)
        return (new_k, new_v), (attended_block, grad_block)

    (acc_keys, acc_values), (attended_blocks, grad_blocks) = lax.scan(advance, (acc_keys, acc_values), jnp.arange(block_total, dtype=jnp.int32))
    attended = attended_blocks.reshape(SEQ_LEN, feat_width)
    grad_queries = grad_blocks.reshape(SEQ_LEN, feat_width)
    inner_k = [x[BLOCK:-BLOCK] for x in acc_keys]
    inner_v = [x[BLOCK:-BLOCK] for x in acc_values]
    for height in range(LEVELS - 1, 0, -1):
        inner_k[height - 1] = inner_k[height - 1] + jnp.repeat(inner_k[height], 2, axis=0) * 0.5
        inner_v[height - 1] = inner_v[height - 1] + jnp.repeat(inner_v[height], 2, axis=0) * 0.5
    return attended, grad_queries, inner_k[0].astype(jnp.bfloat16), inner_v[0].astype(jnp.bfloat16)
```

```python
import math

import jax
import jax.numpy as jnp
from jax import lax
from jax.experimental import pallas as pl
from jax.experimental.pallas import tpu as pltpu
from jax.sharding import PartitionSpec as P

HEADS = 16
HEAD_DIM = 128
BLOCK = 64
HALF = BLOCK // 2
CHUNKS = 4

SIB_FINE = 2 * BLOCK
OUT_FINE = SIB_FINE + BLOCK
OWN_L1 = OUT_FINE + BLOCK
OWN_L2 = OWN_L1 + BLOCK
SIB_L1 = OWN_L2 + HALF
SIB_L2 = SIB_L1 + BLOCK
OUT_L1 = SIB_L2 + HALF
OUT_L2 = OUT_L1 + BLOCK
FAR_L2 = OUT_L2 + BLOCK
CAND = FAR_L2 + BLOCK
COARSE = BLOCK + HALF
BACK = BLOCK + COARSE + BLOCK
FWD = BLOCK + HALF + HALF

masked_score = -1e30
MESH = pl.DeviceIdType.MESH


def nt(a, b):
    return lax.dot_general(a, b, (((1,), (1,)), ((), ())), preferred_element_type=jnp.float32)


def nn(a, b):
    return lax.dot_general(a, b, (((1,), (0,)), ((), ())), preferred_element_type=jnp.float32)


def tn(a, b):
    return lax.dot_general(a, b, (((0,), (0,)), ((), ())), preferred_element_type=jnp.float32)


def pool_matrix(rows):
    row = lax.broadcasted_iota(jnp.int32, (rows // 2, rows), 0)
    col = lax.broadcasted_iota(jnp.int32, (rows // 2, rows), 1)
    return jnp.where((col >> 1) == row, 0.5, 0.0).astype(jnp.bfloat16)


def spread_matrix(rows):
    row = lax.broadcasted_iota(jnp.int32, (2 * rows, rows), 0)
    col = lax.broadcasted_iota(jnp.int32, (2 * rows, rows), 1)
    return jnp.where((row >> 1) == col, 0.5, 0.0).astype(jnp.bfloat16)


def pooled(rows):
    return nn(pool_matrix(rows.shape[0]), rows).astype(jnp.bfloat16)


def spread(grads):
    matrix = spread_matrix(grads.shape[0])
    high = grads.astype(jnp.bfloat16)
    low = (grads - high.astype(jnp.float32)).astype(jnp.bfloat16)
    return nn(matrix, high) + nn(matrix, low)


def kernel(q_ref, k_ref, v_ref, do_ref, att_ref, gq_ref, gk_ref, gv_ref,
           kv, grad, bias, back_out, back_in, ret_out, ret_in, last_in, send_sem, recv_sem):
    count = lax.axis_size("seq")
    me = lax.axis_index("seq")
    side = lax.rem(me, 2)
    sib = me + 1 - 2 * side
    outer = me - 1 + 2 * side
    has_outer = (outer >= 0) & (outer < count)
    sib_outer = sib + 1 - 2 * side
    has_far = (sib_outer >= 0) & (sib_outer < count)
    feat = q_ref.shape[1]
    width = feat // CHUNKS
    scale = HEAD_DIM ** -0.5
    inner_start = pl.multiple_of(BLOCK * (1 - side), BLOCK)
    outer_start = pl.multiple_of(BLOCK * side, BLOCK)
    inner_half = pl.multiple_of(HALF * (1 - side), HALF)

    barrier = pltpu.get_barrier_semaphore()
    pl.semaphore_signal(barrier, inc=1, device_id={"seq": sib}, device_id_type=MESH)

    @pl.when(has_outer)
    def _():
        pl.semaphore_signal(barrier, inc=1, device_id={"seq": outer}, device_id_type=MESH)

    own = pl.ds(0, 2 * BLOCK)
    for which, ref in enumerate((k_ref, v_ref)):
        kv[which, own, :] = ref[...]
        first = pooled(ref[...])
        kv[which, OWN_L1:OWN_L1 + BLOCK, :] = first
        kv[which, OWN_L2:OWN_L2 + HALF, :] = pooled(first)

    @pl.when(jnp.logical_not(has_outer))
    def _():
        for which in range(2):
            kv[which, OUT_FINE:OUT_FINE + BLOCK, :] = jnp.zeros((BLOCK, feat), jnp.bfloat16)
            kv[which, OUT_L1:OUT_L1 + 2 * BLOCK, :] = jnp.zeros((2 * BLOCK, feat), jnp.bfloat16)

    lane = lax.broadcasted_iota(jnp.int32, (BLOCK, 2 * BLOCK), 1)
    is_outer_lane = (lane >> 6) == side
    zero = jnp.zeros((BLOCK, 2 * BLOCK), jnp.float32)
    bias[0:BLOCK] = zero
    bias[BLOCK:2 * BLOCK] = zero
    bias[SIB_FINE:SIB_FINE + BLOCK] = jnp.where(is_outer_lane, masked_score, zero)
    bias[OUT_FINE:OUT_FINE + BLOCK] = jnp.where(is_outer_lane & has_outer, zero, masked_score)
    bias[OWN_L1:OWN_L1 + BLOCK] = zero + 1.0
    bias[OWN_L2:OWN_L2 + HALF] = zero[:HALF] + 2.0
    bias[SIB_L1:SIB_L1 + BLOCK] = zero + 1.0
    bias[SIB_L2:SIB_L2 + HALF] = zero[:HALF] + 2.0
    bias[OUT_L1:OUT_L1 + BLOCK] = jnp.where(has_outer, zero + 1.0, masked_score)
    bias[OUT_L2:OUT_L2 + BLOCK] = jnp.where(has_outer, zero + 2.0, masked_score)
    bias[FAR_L2:FAR_L2 + BLOCK] = jnp.where(has_far, zero + 2.0, masked_score)

    @pl.when(has_outer)
    def _():
        pl.semaphore_wait(barrier, 2)

    @pl.when(jnp.logical_not(has_outer))
    def _():
        pl.semaphore_wait(barrier, 1)

    def part(ref, row, rows, chunk):
        return ref.at[:, pl.ds(row, rows), pl.ds(chunk * width, width)]

    def copy(stage, chunk, src, src_row, dst, dst_row, rows, target):
        return pltpu.make_async_remote_copy(
            src_ref=part(src, src_row, rows, chunk),
            dst_ref=part(dst, dst_row, rows, chunk),
            send_sem=send_sem.at[stage, chunk],
            recv_sem=recv_sem.at[stage, chunk],
            device_id={"seq": target},
            device_id_type=MESH,
        )

    def sib_fine(g):
        return copy(0, g, kv, inner_start, kv, SIB_FINE, BLOCK, sib)

    def sib_coarse(g):
        return copy(1, g, kv, OWN_L1, kv, SIB_L1, COARSE, sib)

    def out_fine(g):
        return copy(2, g, kv, outer_start, kv, OUT_FINE, BLOCK, outer)

    def out_l1(g):
        return copy(3, g, kv, OWN_L1 + inner_half, kv, OUT_L1 + HALF, HALF, outer)

    def out_l2(g):
        return copy(4, g, kv, SIB_L2, kv, OUT_L2 + HALF, HALF, outer)

    def far(g):
        return copy(5, g, kv, OUT_L2, kv, FAR_L2, BLOCK, sib)

    def back(g):
        return copy(6, g, back_out, 0, back_in, 0, BACK, sib)

    def ret(g):
        return copy(7, g, ret_out, 0, ret_in, 0, FWD, outer)

    def last(g):
        return copy(8, g, ret_in, BLOCK + HALF, last_in, 0, HALF, sib)

    for g in range(CHUNKS):
        sib_coarse(g).start()
        sib_fine(g).start()
    for g in range(CHUNKS):
        @pl.when(has_outer)
        def _():
            out_fine(g).start()
            out_l1(g).start()
        sib_coarse(g).wait_recv()

        @pl.when(has_outer)
        def _():
            out_l2(g).start()

    def relay_far(g):
        cols = pl.ds(g * width, width)

        @pl.when(has_outer)
        def _():
            out_fine(g).wait_recv()
            out_l1(g).wait_recv()
            out_l2(g).wait_recv()
            for which in range(2):
                first = pooled(kv[which, pl.ds(OUT_FINE, BLOCK), cols])
                kv[which, pl.ds(OUT_L1, HALF), cols] = first
                second = pooled(kv[which, pl.ds(OUT_L1, BLOCK), cols])
                kv[which, pl.ds(OUT_L2, HALF), cols] = second
        far(g).start()

    def attend(h):
        cols = pl.ds(pl.multiple_of(h * HEAD_DIM, HEAD_DIM), HEAD_DIM)
        q = q_ref[:, cols]
        do = do_ref[:, cols]
        k = kv[0, :, cols]
        v = kv[1, :, cols]
        scores = nt(k, q) * (scale * math.log2(math.e)) + bias[...]
        largest = jnp.max(scores, axis=0, keepdims=True)
        raised = jnp.exp2(scores - largest)
        weights = raised * (1.0 / jnp.sum(raised, axis=0, keepdims=True))
        weights_b = weights.astype(jnp.bfloat16)
        attended = tn(weights_b, v).astype(jnp.bfloat16)
        att_ref[:, cols] = attended
        product = do.astype(jnp.float32) * attended.astype(jnp.float32)
        row_dots = jnp.sum(product.T, axis=0, keepdims=True)
        grad_scores = (weights * (nt(v, do) - row_dots) * scale).astype(jnp.bfloat16)
        gq_ref[:, cols] = tn(grad_scores, k).astype(jnp.bfloat16)
        grad[0, :, cols] = nn(grad_scores, q)
        grad[1, :, cols] = nn(weights_b, do)

    def send_back(g):
        cols = pl.ds(g * width, width)
        for which in range(2):
            for dst, src, rows in ((0, SIB_FINE, BLOCK), (BLOCK, SIB_L1, COARSE),
                                   (BLOCK + COARSE, FAR_L2, BLOCK)):
                back_out[which, pl.ds(dst, rows), cols] = (
                    grad[which, pl.ds(src, rows), cols].astype(jnp.bfloat16))
        back(g).start()

    def send_outer(g):
        cols = pl.ds(g * width, width)
        back(g).wait_recv()
        for which in range(2):
            def take(row, rows):
                return back_in[which, pl.ds(row, rows), cols].astype(jnp.float32)
            rows = pl.ds(inner_start, BLOCK)
            grad[which, rows, cols] += take(0, BLOCK)
            rows = pl.ds(OWN_L1, COARSE)
            grad[which, rows, cols] += take(BLOCK, COARSE)

        @pl.when(has_outer)
        def _():
            for which in range(2):
                second = (grad[which, pl.ds(OUT_L2, BLOCK), cols]
                          + back_in[which, pl.ds(BLOCK + COARSE, BLOCK), cols].astype(jnp.float32))
                first = grad[which, pl.ds(OUT_L1, BLOCK), cols] + spread(second[:HALF])
                fine = grad[which, pl.ds(OUT_FINE, BLOCK), cols] + spread(first[:HALF])
                ret_out[which, pl.ds(0, BLOCK), cols] = fine.astype(jnp.bfloat16)
                ret_out[which, pl.ds(BLOCK, HALF), cols] = first[HALF:].astype(jnp.bfloat16)
                ret_out[which, pl.ds(BLOCK + HALF, HALF), cols] = second[HALF:].astype(jnp.bfloat16)
            ret(g).start()

    def take_outer(g):
        cols = pl.ds(g * width, width)

        @pl.when(has_outer)
        def _():
            ret(g).wait_recv()
            last(g).start()
            for which in range(2):
                rows = pl.ds(outer_start, BLOCK)
                grad[which, rows, cols] += ret_in[which, pl.ds(0, BLOCK), cols].astype(jnp.float32)
                rows = pl.ds(OWN_L1 + inner_half, HALF)
                grad[which, rows, cols] += ret_in[which, pl.ds(BLOCK, HALF), cols].astype(jnp.float32)

    def finish(g):
        cols = pl.ds(g * width, width)

        @pl.when(has_far)
        def _():
            last(g).wait_recv()
            for which in range(2):
                rows = pl.ds(OWN_L2, HALF)
                grad[which, rows, cols] += last_in[which, :, cols].astype(jnp.float32)
        for which, ref in enumerate((gk_ref, gv_ref)):
            first = grad[which, pl.ds(OWN_L1, BLOCK), cols] + spread(grad[which, pl.ds(OWN_L2, HALF), cols])
            fine = grad[which, pl.ds(0, 2 * BLOCK), cols] + spread(first)
            ref[:, cols] = fine.astype(jnp.bfloat16)

    heads = width // HEAD_DIM
    for g in range(CHUNKS):
        relay_far(g)
        sib_fine(g).wait_recv()
        far(g).wait_recv()
        lax.fori_loop(g * heads, (g + 1) * heads, lambda h, c: (attend(h), c)[1], 0)
        send_back(g)
        if g > 0:
            send_outer(g - 1)
    send_outer(CHUNKS - 1)
    for g in range(CHUNKS):
        take_outer(g)
        if g > 0:
            finish(g - 1)
    finish(CHUNKS - 1)
    for g in range(CHUNKS):
        for item in (sib_fine, sib_coarse, far, back):
            item(g).wait_send()

        @pl.when(has_outer)
        def _():
            for item in (out_fine, out_l1, out_l2, ret, last):
                item(g).wait_send()


def body(queries, key_input, value_input, cotangent):
    rows, feat = queries.shape
    out = jax.ShapeDtypeStruct((rows, feat), jnp.bfloat16)
    return tuple(pl.pallas_call(
        kernel,
        name="hier_attention",
        out_shape=[out] * 4,
        in_specs=[pl.BlockSpec(memory_space=pltpu.VMEM)] * 4,
        out_specs=[pl.BlockSpec(memory_space=pltpu.VMEM)] * 4,
        scratch_shapes=[
            pltpu.VMEM((2, CAND, feat), jnp.bfloat16),
            pltpu.VMEM((2, CAND, feat), jnp.float32),
            pltpu.VMEM((CAND, rows), jnp.float32),
            pltpu.VMEM((2, BACK, feat), jnp.bfloat16),
            pltpu.VMEM((2, BACK, feat), jnp.bfloat16),
            pltpu.VMEM((2, FWD, feat), jnp.bfloat16),
            pltpu.VMEM((2, FWD, feat), jnp.bfloat16),
            pltpu.VMEM((2, HALF, feat), jnp.bfloat16),
            pltpu.SemaphoreType.DMA((9, CHUNKS)),
            pltpu.SemaphoreType.DMA((9, CHUNKS)),
        ],
        compiler_params=pltpu.CompilerParams(
            collective_id=0, has_side_effects=True, vmem_limit_bytes=56 * 1024 * 1024),
    )(queries, key_input, value_input, cotangent))


def solution(mesh):
    spec = P(("groups", "seq"), None)
    return jax.shard_map(
        body, mesh=mesh, in_specs=(spec,) * 4, out_specs=(spec,) * 4, check_vma=False)
```

```python
import math

import jax
import jax.numpy as jnp
from jax import lax
from jax.experimental import pallas as pl
from jax.experimental.pallas import tpu as pltpu
from jax.sharding import PartitionSpec as P

HEADS = 16
HEAD_DIM = 128
BLOCK = 64
HALF = BLOCK // 2
CHUNKS = 8

SIB_FINE = 2 * BLOCK
OUT_FINE = SIB_FINE + BLOCK
OWN_L1 = OUT_FINE + BLOCK
OWN_L2 = OWN_L1 + BLOCK
SIB_L1 = OWN_L2 + HALF
SIB_L2 = SIB_L1 + BLOCK
OUT_L1 = SIB_L2 + HALF
OUT_L2 = OUT_L1 + BLOCK
FAR_L2 = OUT_L2 + BLOCK
CAND = FAR_L2 + BLOCK
COARSE = BLOCK + HALF
BACK = BLOCK + COARSE + BLOCK
RET = BLOCK + HALF
RELAY_L1 = BLOCK
RELAY_L2 = 2 * BLOCK
RELAY = RELAY_L2 + HALF
STAGES = 14

masked_score = -1e30
MESH = pl.DeviceIdType.MESH


def nt(a, b):
    return lax.dot_general(a, b, (((1,), (1,)), ((), ())), preferred_element_type=jnp.float32)


def nn(a, b):
    return lax.dot_general(a, b, (((1,), (0,)), ((), ())), preferred_element_type=jnp.float32)


def tn(a, b):
    return lax.dot_general(a, b, (((0,), (0,)), ((), ())), preferred_element_type=jnp.float32)


def pool_matrix(rows):
    row = lax.broadcasted_iota(jnp.int32, (rows // 2, rows), 0)
    col = lax.broadcasted_iota(jnp.int32, (rows // 2, rows), 1)
    return jnp.where((col >> 1) == row, 0.5, 0.0).astype(jnp.bfloat16)


def spread_matrix(rows):
    row = lax.broadcasted_iota(jnp.int32, (2 * rows, rows), 0)
    col = lax.broadcasted_iota(jnp.int32, (2 * rows, rows), 1)
    return jnp.where((row >> 1) == col, 0.5, 0.0).astype(jnp.bfloat16)


def pooled(rows):
    return nn(pool_matrix(rows.shape[0]), rows).astype(jnp.bfloat16)


def spread(grads):
    matrix = spread_matrix(grads.shape[0])
    high = grads.astype(jnp.bfloat16)
    low = (grads - high.astype(jnp.float32)).astype(jnp.bfloat16)
    return nn(matrix, high) + nn(matrix, low)


def kernel(q_ref, k_ref, v_ref, do_ref, att_ref, gq_ref, gk_ref, gv_ref,
           kv, grad, bias, relay, back_out, back_in, z_out, z_in, s_out, s_in,
           ret_out, ret_in, send_sem, recv_sem):
    count = lax.axis_size("seq")
    me = lax.axis_index("seq")
    side = lax.rem(me, 2)
    chip = me // 2
    odd = lax.rem(chip, 2)
    sib = me + 1 - 2 * side
    is_p = lax.rem(side + chip, 2) == 1
    is_d = jnp.logical_not(is_p)
    peer = 2 * (chip + 1 - 2 * odd) + 1 - side
    step = 4 - 8 * odd
    has_next = (me + step >= 0) & (me + step < count)
    has_prev = (me - step >= 0) & (me - step < count)
    has_outer = is_p | has_prev
    has_far = is_d | has_prev
    d_next = is_d & has_next
    d_prev = is_d & has_prev
    p_next = is_p & has_next
    feat = q_ref.shape[1]
    width = feat // CHUNKS
    scale = HEAD_DIM ** -0.5
    inner_start = pl.multiple_of(BLOCK * (1 - side), BLOCK)
    outer_start = pl.multiple_of(BLOCK * side, BLOCK)
    inner_half = pl.multiple_of(HALF * (1 - side), HALF)

    barrier = pltpu.get_barrier_semaphore()

    def greet(target):
        pl.semaphore_signal(barrier, inc=1, device_id={"seq": target}, device_id_type=MESH)

    greet(sib)
    greet(peer)

    @pl.when(d_next)
    def _():
        greet(me + step)

    @pl.when(p_next)
    def _():
        greet(sib + step)

    @pl.when(d_prev)
    def _():
        greet(me - step)
        greet(sib - step)

    own = pl.ds(0, 2 * BLOCK)
    for which, ref in enumerate((k_ref, v_ref)):
        kv[which, own, :] = ref[...]
        first = pooled(ref[...])
        kv[which, OWN_L1:OWN_L1 + BLOCK, :] = first
        kv[which, OWN_L2:OWN_L2 + HALF, :] = pooled(first)

    @pl.when(jnp.logical_not(has_outer))
    def _():
        for which in range(2):
            kv[which, OUT_FINE:OUT_FINE + BLOCK, :] = jnp.zeros((BLOCK, feat), jnp.bfloat16)
            kv[which, OUT_L1:OUT_L1 + 2 * BLOCK, :] = jnp.zeros((2 * BLOCK, feat), jnp.bfloat16)

    @pl.when(is_d & jnp.logical_not(has_next))
    def _():
        z_in[:, 0:RET, :] = jnp.zeros((2, RET, feat), jnp.bfloat16)

    lane = lax.broadcasted_iota(jnp.int32, (BLOCK, 2 * BLOCK), 1)
    is_outer_lane = (lane >> 6) == side
    zero = jnp.zeros((BLOCK, 2 * BLOCK), jnp.float32)
    bias[0:BLOCK] = zero
    bias[BLOCK:2 * BLOCK] = zero
    bias[SIB_FINE:SIB_FINE + BLOCK] = jnp.where(is_outer_lane, masked_score, zero)
    bias[OUT_FINE:OUT_FINE + BLOCK] = jnp.where(is_outer_lane & has_outer, zero, masked_score)
    bias[OWN_L1:OWN_L1 + BLOCK] = zero + 1.0
    bias[OWN_L2:OWN_L2 + HALF] = zero[:HALF] + 2.0
    bias[SIB_L1:SIB_L1 + BLOCK] = zero + 1.0
    bias[SIB_L2:SIB_L2 + HALF] = zero[:HALF] + 2.0
    bias[OUT_L1:OUT_L1 + BLOCK] = jnp.where(has_outer, zero + 1.0, masked_score)
    bias[OUT_L2:OUT_L2 + BLOCK] = jnp.where(has_outer, zero + 2.0, masked_score)
    bias[FAR_L2:FAR_L2 + BLOCK] = jnp.where(has_far, zero + 2.0, masked_score)

    peers = 2 + has_next.astype(jnp.int32) + 2 * d_prev.astype(jnp.int32)
    pl.semaphore_wait(barrier, peers)

    def copy(stage, chunk, src, src_row, dst, dst_row, rows, target):
        cols = pl.ds(chunk * width, width)
        return pltpu.make_async_remote_copy(
            src_ref=src.at[:, pl.ds(src_row, rows), cols],
            dst_ref=dst.at[:, pl.ds(dst_row, rows), cols],
            send_sem=send_sem.at[stage, chunk],
            recv_sem=recv_sem.at[stage, chunk],
            device_id={"seq": target},
            device_id_type=MESH,
        )

    def sib_fine(g):
        return copy(0, g, kv, inner_start, kv, SIB_FINE, BLOCK, sib)

    def sib_coarse(g):
        return copy(1, g, kv, OWN_L1, kv, SIB_L1, COARSE, sib)

    def p_fine(g):
        return copy(2, g, kv, outer_start, kv, OUT_FINE, BLOCK, peer)

    def p_l1(g):
        return copy(3, g, kv, OWN_L1 + inner_half, kv, OUT_L1 + HALF, HALF, peer)

    def d_fine(g):
        return copy(2, g, kv, outer_start, relay, 0, BLOCK, peer)

    def d_l1(g):
        return copy(3, g, kv, OWN_L1 + inner_half, relay, RELAY_L1 + HALF, HALF, peer)

    def z_fine(g):
        return copy(4, g, relay, 0, kv, OUT_FINE, BLOCK, me + step)

    def z_l1(g):
        return copy(5, g, relay, RELAY_L1 + HALF, kv, OUT_L1 + HALF, HALF, me + step)

    def z_l2(g):
        return copy(6, g, kv, OUT_L2, kv, OUT_L2 + HALF, HALF, sib + step)

    def sib_l2(g):
        return copy(7, g, relay, RELAY_L2, kv, OUT_L2 + HALF, HALF, sib)

    def far(g):
        return copy(8, g, kv, OUT_L2, kv, FAR_L2, BLOCK, sib)

    def back(g):
        return copy(9, g, back_out, 0, back_in, 0, BACK, sib)

    def z_main(g):
        return copy(10, g, z_out, 0, z_in, 0, RET, me - step)

    def z_grad2(g):
        return copy(11, g, z_out, RET, z_in, RET, HALF, sib - step)

    def sib_grad2(g):
        return copy(12, g, s_out, 0, s_in, 0, HALF, sib)

    def ret(g):
        return copy(13, g, ret_out, 0, ret_in, 0, RET, peer)

    for g in range(CHUNKS):
        @pl.when(is_p)
        def _():
            p_fine(g).start()
            p_l1(g).start()

        @pl.when(is_d)
        def _():
            d_fine(g).start()
            d_l1(g).start()
        sib_coarse(g).start()
        sib_fine(g).start()

    def derive(ref, which, cols, fine, first, second):
        ref[which, pl.ds(first, HALF), cols] = pooled(ref[which, pl.ds(fine, BLOCK), cols])
        ref[which, pl.ds(second, HALF), cols] = pooled(ref[which, pl.ds(first, BLOCK), cols])

    def forward(g):
        cols = pl.ds(g * width, width)

        @pl.when(is_p)
        def _():
            p_fine(g).wait_recv()
            p_l1(g).wait_recv()
            for which in range(2):
                derive(kv, which, cols, OUT_FINE, OUT_L1, OUT_L2)

        @pl.when(p_next)
        def _():
            z_l2(g).start()

        @pl.when(is_d)
        def _():
            d_fine(g).wait_recv()
            d_l1(g).wait_recv()

        @pl.when(d_next)
        def _():
            z_fine(g).start()
            z_l1(g).start()

        @pl.when(is_d)
        def _():
            for which in range(2):
                derive(relay, which, cols, 0, RELAY_L1, RELAY_L2)
            sib_l2(g).start()

    def share_far(g):
        cols = pl.ds(g * width, width)

        @pl.when(is_p)
        def _():
            sib_l2(g).wait_recv()

        @pl.when(d_prev)
        def _():
            z_fine(g).wait_recv()
            z_l1(g).wait_recv()
            for which in range(2):
                derive(kv, which, cols, OUT_FINE, OUT_L1, OUT_L2)
            z_l2(g).wait_recv()
        far(g).start()

    def attend(h):
        cols = pl.ds(pl.multiple_of(h * HEAD_DIM, HEAD_DIM), HEAD_DIM)
        q = q_ref[:, cols]
        do = do_ref[:, cols]
        k = kv[0, :, cols]
        v = kv[1, :, cols]
        scores = nt(k, q) * (scale * math.log2(math.e)) + bias[...]
        largest = jnp.max(scores, axis=0, keepdims=True)
        raised = jnp.exp2(scores - largest)
        weights = raised * (1.0 / jnp.sum(raised, axis=0, keepdims=True))
        weights_b = weights.astype(jnp.bfloat16)
        attended = tn(weights_b, v).astype(jnp.bfloat16)
        att_ref[:, cols] = attended
        product = do.astype(jnp.float32) * attended.astype(jnp.float32)
        row_dots = jnp.sum(product.T, axis=0, keepdims=True)
        grad_scores = (weights * (nt(v, do) - row_dots) * scale).astype(jnp.bfloat16)
        gq_ref[:, cols] = tn(grad_scores, k).astype(jnp.bfloat16)
        grad[0, :, cols] = nn(grad_scores, q)
        grad[1, :, cols] = nn(weights_b, do)

    def send_back(g):
        cols = pl.ds(g * width, width)
        for which in range(2):
            for dst, src, rows in ((0, SIB_FINE, BLOCK), (BLOCK, SIB_L1, COARSE),
                                   (BLOCK + COARSE, FAR_L2, BLOCK)):
                back_out[which, pl.ds(dst, rows), cols] = (
                    grad[which, pl.ds(src, rows), cols].astype(jnp.bfloat16))
        back(g).start()

    def send_outer(g):
        cols = pl.ds(g * width, width)
        back(g).wait_recv()
        for which in range(2):
            def take(row, rows):
                return back_in[which, pl.ds(row, rows), cols].astype(jnp.float32)
            rows = pl.ds(inner_start, BLOCK)
            grad[which, rows, cols] += take(0, BLOCK)
            rows = pl.ds(OWN_L1, COARSE)
            grad[which, rows, cols] += take(BLOCK, COARSE)
            rows = pl.ds(OUT_L2, BLOCK)
            grad[which, rows, cols] += take(BLOCK + COARSE, BLOCK)

        @pl.when(d_prev)
        def _():
            for which in range(2):
                second = grad[which, pl.ds(OUT_L2, BLOCK), cols]
                first = grad[which, pl.ds(OUT_L1, BLOCK), cols] + spread(second[:HALF])
                fine = grad[which, pl.ds(OUT_FINE, BLOCK), cols] + spread(first[:HALF])
                z_out[which, pl.ds(0, BLOCK), cols] = fine.astype(jnp.bfloat16)
                z_out[which, pl.ds(BLOCK, HALF), cols] = first[HALF:].astype(jnp.bfloat16)
                z_out[which, pl.ds(RET, HALF), cols] = second[HALF:].astype(jnp.bfloat16)
            z_main(g).start()
            z_grad2(g).start()

        @pl.when(is_p)
        def _():
            for which in range(2):
                s_out[which, :, cols] = grad[which, pl.ds(OUT_L2 + HALF, HALF), cols].astype(jnp.bfloat16)
            sib_grad2(g).start()

    def send_peer(g):
        cols = pl.ds(g * width, width)

        @pl.when(p_next)
        def _():
            z_grad2(g).wait_recv()
            for which in range(2):
                grad[which, pl.ds(OUT_L2, HALF), cols] += (
                    z_in[which, pl.ds(RET, HALF), cols].astype(jnp.float32))

        @pl.when(is_p)
        def _():
            for which in range(2):
                first = (grad[which, pl.ds(OUT_L1, BLOCK), cols]
                         + spread(grad[which, pl.ds(OUT_L2, HALF), cols]))
                fine = grad[which, pl.ds(OUT_FINE, BLOCK), cols] + spread(first[:HALF])
                ret_out[which, pl.ds(0, BLOCK), cols] = fine.astype(jnp.bfloat16)
                ret_out[which, pl.ds(BLOCK, HALF), cols] = first[HALF:].astype(jnp.bfloat16)

        @pl.when(d_next)
        def _():
            z_main(g).wait_recv()

        @pl.when(is_d)
        def _():
            sib_grad2(g).wait_recv()
            for which in range(2):
                first = spread(s_in[which, :, cols].astype(jnp.float32))
                fine = spread(first[:HALF])
                fine += z_in[which, pl.ds(0, BLOCK), cols].astype(jnp.float32)
                rest = first[HALF:] + z_in[which, pl.ds(BLOCK, HALF), cols].astype(jnp.float32)
                ret_out[which, pl.ds(0, BLOCK), cols] = fine.astype(jnp.bfloat16)
                ret_out[which, pl.ds(BLOCK, HALF), cols] = rest.astype(jnp.bfloat16)
        ret(g).start()

    def finish(g):
        cols = pl.ds(g * width, width)
        ret(g).wait_recv()
        for which, ref in enumerate((gk_ref, gv_ref)):
            rows = pl.ds(outer_start, BLOCK)
            grad[which, rows, cols] += ret_in[which, pl.ds(0, BLOCK), cols].astype(jnp.float32)
            rows = pl.ds(OWN_L1 + inner_half, HALF)
            grad[which, rows, cols] += ret_in[which, pl.ds(BLOCK, HALF), cols].astype(jnp.float32)
            first = grad[which, pl.ds(OWN_L1, BLOCK), cols] + spread(grad[which, pl.ds(OWN_L2, HALF), cols])
            fine = grad[which, pl.ds(0, 2 * BLOCK), cols] + spread(first)
            ref[:, cols] = fine.astype(jnp.bfloat16)

    heads = width // HEAD_DIM
    forward(0)
    for g in range(CHUNKS):
        if g + 1 < CHUNKS:
            forward(g + 1)
        share_far(g)
        sib_coarse(g).wait_recv()
        sib_fine(g).wait_recv()
        far(g).wait_recv()
        lax.fori_loop(g * heads, (g + 1) * heads, lambda h, c: (attend(h), c)[1], 0)
        send_back(g)
        if g > 0:
            send_outer(g - 1)
        if g > 1:
            send_peer(g - 2)
    send_outer(CHUNKS - 1)
    for g in range(max(0, CHUNKS - 2), CHUNKS):
        send_peer(g)
    for g in range(CHUNKS):
        finish(g)
    for g in range(CHUNKS):
        for item in (sib_fine, sib_coarse, p_fine, p_l1, far, back, ret):
            item(g).wait_send()

        @pl.when(is_p)
        def _():
            sib_grad2(g).wait_send()

        @pl.when(is_d)
        def _():
            sib_l2(g).wait_send()

        @pl.when(p_next)
        def _():
            z_l2(g).wait_send()

        @pl.when(d_next)
        def _():
            z_fine(g).wait_send()
            z_l1(g).wait_send()

        @pl.when(d_prev)
        def _():
            z_main(g).wait_send()
            z_grad2(g).wait_send()


def body(queries, key_input, value_input, cotangent):
    rows, feat = queries.shape
    out = jax.ShapeDtypeStruct((rows, feat), jnp.bfloat16)
    return tuple(pl.pallas_call(
        kernel,
        name="hier_attention",
        out_shape=[out] * 4,
        in_specs=[pl.BlockSpec(memory_space=pltpu.VMEM)] * 4,
        out_specs=[pl.BlockSpec(memory_space=pltpu.VMEM)] * 4,
        scratch_shapes=[
            pltpu.VMEM((2, CAND, feat), jnp.bfloat16),
            pltpu.VMEM((2, CAND, feat), jnp.float32),
            pltpu.VMEM((CAND, rows), jnp.float32),
            pltpu.VMEM((2, RELAY, feat), jnp.bfloat16),
            pltpu.VMEM((2, BACK, feat), jnp.bfloat16),
            pltpu.VMEM((2, BACK, feat), jnp.bfloat16),
            pltpu.VMEM((2, RET + HALF, feat), jnp.bfloat16),
            pltpu.VMEM((2, RET + HALF, feat), jnp.bfloat16),
            pltpu.VMEM((2, HALF, feat), jnp.bfloat16),
            pltpu.VMEM((2, HALF, feat), jnp.bfloat16),
            pltpu.VMEM((2, RET, feat), jnp.bfloat16),
            pltpu.VMEM((2, RET, feat), jnp.bfloat16),
            pltpu.SemaphoreType.DMA((STAGES, CHUNKS)),
            pltpu.SemaphoreType.DMA((STAGES, CHUNKS)),
        ],
        compiler_params=pltpu.CompilerParams(
            collective_id=0, has_side_effects=True, vmem_limit_bytes=56 * 1024 * 1024),
    )(queries, key_input, value_input, cotangent))


def solution(mesh):
    spec = P(("groups", "seq"), None)
    return jax.shard_map(
        body, mesh=mesh, in_specs=(spec,) * 4, out_specs=(spec,) * 4, check_vma=False)
```

```python
import math

import jax
import jax.numpy as jnp
from jax import lax
from jax.experimental import pallas as pl
from jax.experimental.pallas import tpu as pltpu
from jax.sharding import PartitionSpec as P

HEADS = 16
HEAD_DIM = 128
BLOCK = 64
HALF = BLOCK // 2
CHUNKS = 8
EARLY = 2
LAG = 8

SIB_FINE = 2 * BLOCK
OUT_FINE = SIB_FINE + BLOCK
OWN_L1 = OUT_FINE + BLOCK
OWN_L2 = OWN_L1 + BLOCK
SIB_L1 = OWN_L2 + HALF
SIB_L2 = SIB_L1 + BLOCK
OUT_L1 = SIB_L2 + HALF
OUT_L2 = OUT_L1 + BLOCK
FAR_L2 = OUT_L2 + BLOCK
CAND = FAR_L2 + BLOCK
COARSE = BLOCK + HALF
BACK = BLOCK + COARSE + BLOCK
RET = BLOCK + HALF
RELAY_L1 = BLOCK
RELAY_L2 = 2 * BLOCK
RELAY = RELAY_L2 + HALF
STAGES = 14

masked_score = -1e30
MESH = pl.DeviceIdType.MESH


def nt(a, b):
    return lax.dot_general(a, b, (((1,), (1,)), ((), ())), preferred_element_type=jnp.float32)


def nn(a, b):
    return lax.dot_general(a, b, (((1,), (0,)), ((), ())), preferred_element_type=jnp.float32)


def tn(a, b):
    return lax.dot_general(a, b, (((0,), (0,)), ((), ())), preferred_element_type=jnp.float32)


def pool_matrix(rows):
    row = lax.broadcasted_iota(jnp.int32, (rows // 2, rows), 0)
    col = lax.broadcasted_iota(jnp.int32, (rows // 2, rows), 1)
    return jnp.where((col >> 1) == row, 0.5, 0.0).astype(jnp.bfloat16)


def pooled(rows):
    return nn(pool_matrix(rows.shape[0]), rows).astype(jnp.bfloat16)


def spread_matrix(shape, row0, col0, rows, shift):
    row = lax.broadcasted_iota(jnp.int32, shape, 0) - row0
    col = lax.broadcasted_iota(jnp.int32, shape, 1) - col0
    hit = (row >= 0) & (row < rows) & ((row >> shift) == col)
    return jnp.where(hit, 0.5 ** shift, 0.0)


def spread(matrix, grads):
    matrix = matrix.astype(jnp.bfloat16)
    high = grads.astype(jnp.bfloat16)
    low = (grads - high.astype(jnp.float32)).astype(jnp.bfloat16)
    return nn(jnp.concatenate([matrix, matrix], axis=1), jnp.concatenate([high, low], axis=0))


def message_matrix():
    shape = (RET, BLOCK)
    return (spread_matrix(shape, 0, 0, BLOCK, 1)
            + spread_matrix(shape, 0, HALF, BLOCK, 2)
            + spread_matrix(shape, BLOCK, HALF + HALF // 2, HALF, 1))


def coarse_matrix():
    shape = (RET, HALF)
    return (spread_matrix(shape, 0, 0, BLOCK, 2)
            + spread_matrix(shape, BLOCK, HALF // 2, HALF, 1)).astype(jnp.bfloat16)


def own_matrix():
    shape = (2 * BLOCK, COARSE)
    return (spread_matrix(shape, 0, 0, 2 * BLOCK, 1)
            + spread_matrix(shape, 0, BLOCK, 2 * BLOCK, 2))


def kernel(q_ref, k_ref, v_ref, do_ref, att_ref, gq_ref, gk_ref, gv_ref,
           kv, grad, bias, relay, back_out, back_in, z_out, z_in, s_out, s_in,
           ret_out, ret_in, send_sem, recv_sem):
    count = lax.axis_size("seq")
    me = lax.axis_index("seq")
    side = lax.rem(me, 2)
    chip = me // 2
    odd = lax.rem(chip, 2)
    sib = me + 1 - 2 * side
    is_p = lax.rem(side + chip, 2) == 1
    is_d = jnp.logical_not(is_p)
    peer = 2 * (chip + 1 - 2 * odd) + 1 - side
    step = 4 - 8 * odd
    has_next = (me + step >= 0) & (me + step < count)
    has_prev = (me - step >= 0) & (me - step < count)
    has_outer = is_p | has_prev
    has_far = is_d | has_prev
    d_next = is_d & has_next
    d_prev = is_d & has_prev
    p_next = is_p & has_next
    feat = q_ref.shape[1]
    width = feat // CHUNKS
    scale = HEAD_DIM ** -0.5
    inner_start = pl.multiple_of(BLOCK * (1 - side), BLOCK)
    outer_start = pl.multiple_of(BLOCK * side, BLOCK)
    inner_half = pl.multiple_of(HALF * (1 - side), HALF)

    barrier = pltpu.get_barrier_semaphore()

    def greet(target):
        pl.semaphore_signal(barrier, inc=1, device_id={"seq": target}, device_id_type=MESH)

    greet(sib)
    greet(peer)

    @pl.when(d_next)
    def _():
        greet(me + step)

    @pl.when(p_next)
    def _():
        greet(sib + step)

    @pl.when(d_prev)
    def _():
        greet(me - step)
        greet(sib - step)

    own = pl.ds(0, 2 * BLOCK)
    for which, ref in enumerate((k_ref, v_ref)):
        kv[which, own, :] = ref[...]

    @pl.when(jnp.logical_not(has_outer))
    def _():
        for which in range(2):
            kv[which, OUT_FINE:OUT_FINE + BLOCK, :] = jnp.zeros((BLOCK, feat), jnp.bfloat16)
            kv[which, OUT_L1:OUT_L1 + 2 * BLOCK, :] = jnp.zeros((2 * BLOCK, feat), jnp.bfloat16)

    @pl.when(is_d & jnp.logical_not(has_next))
    def _():
        z_in[:, 0:RET, :] = jnp.zeros((2, RET, feat), jnp.bfloat16)

    lane = lax.broadcasted_iota(jnp.int32, (BLOCK, 2 * BLOCK), 1)
    is_outer_lane = (lane >> 6) == side
    zero = jnp.zeros((BLOCK, 2 * BLOCK), jnp.float32)
    bias[0:BLOCK] = zero
    bias[BLOCK:2 * BLOCK] = zero
    bias[SIB_FINE:SIB_FINE + BLOCK] = jnp.where(is_outer_lane, masked_score, zero)
    bias[OUT_FINE:OUT_FINE + BLOCK] = jnp.where(is_outer_lane & has_outer, zero, masked_score)
    bias[OWN_L1:OWN_L1 + BLOCK] = zero + 1.0
    bias[OWN_L2:OWN_L2 + HALF] = zero[:HALF] + 2.0
    bias[SIB_L1:SIB_L1 + BLOCK] = zero + 1.0
    bias[SIB_L2:SIB_L2 + HALF] = zero[:HALF] + 2.0
    bias[OUT_L1:OUT_L1 + BLOCK] = jnp.where(has_outer, zero + 1.0, masked_score)
    bias[OUT_L2:OUT_L2 + BLOCK] = jnp.where(has_outer, zero + 2.0, masked_score)
    bias[FAR_L2:FAR_L2 + BLOCK] = jnp.where(has_far, zero + 2.0, masked_score)

    peers = 2 + has_next.astype(jnp.int32) + 2 * d_prev.astype(jnp.int32)
    pl.semaphore_wait(barrier, peers)

    def copy(stage, chunk, src, src_row, dst, dst_row, rows, target):
        cols = pl.ds(chunk * width, width)
        return pltpu.make_async_remote_copy(
            src_ref=src.at[:, pl.ds(src_row, rows), cols],
            dst_ref=dst.at[:, pl.ds(dst_row, rows), cols],
            send_sem=send_sem.at[stage, chunk],
            recv_sem=recv_sem.at[stage, chunk],
            device_id={"seq": target},
            device_id_type=MESH,
        )

    def sib_fine(g):
        return copy(0, g, kv, inner_start, kv, SIB_FINE, BLOCK, sib)

    def sib_coarse(g):
        return copy(1, g, kv, OWN_L1, kv, SIB_L1, COARSE, sib)

    def p_fine(g):
        return copy(2, g, kv, outer_start, kv, OUT_FINE, BLOCK, peer)

    def p_l1(g):
        return copy(3, g, kv, OWN_L1 + inner_half, kv, OUT_L1 + HALF, HALF, peer)

    def d_fine(g):
        return copy(2, g, kv, outer_start, relay, 0, BLOCK, peer)

    def d_l1(g):
        return copy(3, g, kv, OWN_L1 + inner_half, relay, RELAY_L1 + HALF, HALF, peer)

    def z_fine(g):
        return copy(4, g, relay, 0, kv, OUT_FINE, BLOCK, me + step)

    def z_l1(g):
        return copy(5, g, relay, RELAY_L1 + HALF, kv, OUT_L1 + HALF, HALF, me + step)

    def z_l2(g):
        return copy(6, g, kv, OUT_L2, kv, OUT_L2 + HALF, HALF, sib + step)

    def sib_l2(g):
        return copy(7, g, relay, RELAY_L2, kv, OUT_L2 + HALF, HALF, sib)

    def far(g):
        return copy(8, g, kv, OUT_L2, kv, FAR_L2, BLOCK, sib)

    def back(g):
        return copy(9, g, back_out, 0, back_in, 0, BACK, sib)

    def z_main(g):
        return copy(10, g, z_out, 0, z_in, 0, RET, me - step)

    def z_grad2(g):
        return copy(11, g, z_out, RET, z_in, RET, HALF, sib - step)

    def sib_grad2(g):
        return copy(12, g, s_out, 0, s_in, 0, HALF, sib)

    def ret(g):
        return copy(13, g, ret_out, 0, ret_in, 0, RET, peer)

    def start_fine(g):
        @pl.when(is_p)
        def _():
            p_fine(g).start()

        @pl.when(is_d)
        def _():
            d_fine(g).start()

    def start_l1(g):
        @pl.when(is_p)
        def _():
            p_l1(g).start()

        @pl.when(is_d)
        def _():
            d_l1(g).start()

    for g in range(EARLY):
        start_fine(g)
    for which in range(2):
        first = pooled(kv[which, own, :])
        kv[which, OWN_L1:OWN_L1 + BLOCK, :] = first
        kv[which, OWN_L2:OWN_L2 + HALF, :] = pooled(first)
    for g in range(CHUNKS):
        if g >= EARLY:
            start_fine(g)
        start_l1(g)
        sib_coarse(g).start()
        sib_fine(g).start()

    def derive(ref, which, cols, fine, first, second):
        ref[which, pl.ds(first, HALF), cols] = pooled(ref[which, pl.ds(fine, BLOCK), cols])
        ref[which, pl.ds(second, HALF), cols] = pooled(ref[which, pl.ds(first, BLOCK), cols])

    def forward(g):
        cols = pl.ds(g * width, width)

        @pl.when(is_p)
        def _():
            p_fine(g).wait_recv()
            p_l1(g).wait_recv()
            for which in range(2):
                derive(kv, which, cols, OUT_FINE, OUT_L1, OUT_L2)

        @pl.when(p_next)
        def _():
            z_l2(g).start()

        @pl.when(is_d)
        def _():
            d_fine(g).wait_recv()
            d_l1(g).wait_recv()

        @pl.when(d_next)
        def _():
            z_fine(g).start()
            z_l1(g).start()

        @pl.when(is_d)
        def _():
            for which in range(2):
                derive(relay, which, cols, 0, RELAY_L1, RELAY_L2)
            sib_l2(g).start()

    def share_far(g):
        cols = pl.ds(g * width, width)

        @pl.when(is_p)
        def _():
            sib_l2(g).wait_recv()

        @pl.when(d_prev)
        def _():
            z_fine(g).wait_recv()
            z_l1(g).wait_recv()
            for which in range(2):
                derive(kv, which, cols, OUT_FINE, OUT_L1, OUT_L2)
            z_l2(g).wait_recv()
        far(g).start()

    def attend(h):
        cols = pl.ds(pl.multiple_of(h * HEAD_DIM, HEAD_DIM), HEAD_DIM)
        q = q_ref[:, cols]
        do = do_ref[:, cols]
        k = kv[0, :, cols]
        v = kv[1, :, cols]
        scores = nt(k, q) * (scale * math.log2(math.e)) + bias[...]
        largest = jnp.max(scores, axis=0, keepdims=True)
        raised = jnp.exp2(scores - largest)
        weights = raised * (1.0 / jnp.sum(raised, axis=0, keepdims=True))
        weights_b = weights.astype(jnp.bfloat16)
        attended = tn(weights_b, v).astype(jnp.bfloat16)
        att_ref[:, cols] = attended
        product = do.astype(jnp.float32) * attended.astype(jnp.float32)
        row_dots = jnp.sum(product.T, axis=0, keepdims=True)
        grad_scores = (weights * (nt(v, do) - row_dots) * scale).astype(jnp.bfloat16)
        gq_ref[:, cols] = tn(grad_scores, k).astype(jnp.bfloat16)
        for which, part in ((0, nn(grad_scores, q)), (1, nn(weights_b, do))):
            for start, end in ((0, SIB_FINE), (OUT_FINE, SIB_L1), (OUT_L1, FAR_L2)):
                grad[which, start:end, cols] = part[start:end]
            for dst, src, rows in ((0, SIB_FINE, BLOCK), (BLOCK, SIB_L1, COARSE),
                                   (BLOCK + COARSE, FAR_L2, BLOCK)):
                back_out[which, dst:dst + rows, cols] = part[src:src + rows].astype(jnp.bfloat16)

    def folded(which, cols):
        coarse = jnp.concatenate([grad[which, pl.ds(OUT_L1, HALF), cols],
                                  grad[which, pl.ds(OUT_L2, HALF), cols]], axis=0)
        total = spread(message_matrix(), coarse)
        total += jnp.concatenate([grad[which, pl.ds(OUT_FINE, BLOCK), cols],
                                  grad[which, pl.ds(OUT_L1 + HALF, HALF), cols]], axis=0)
        return total.astype(jnp.bfloat16)

    def send_outer(g):
        cols = pl.ds(g * width, width)
        back(g).wait_recv()
        for which in range(2):
            def take(row, rows):
                return back_in[which, pl.ds(row, rows), cols].astype(jnp.float32)
            rows = pl.ds(inner_start, BLOCK)
            grad[which, rows, cols] += take(0, BLOCK)
            rows = pl.ds(OWN_L1, COARSE)
            grad[which, rows, cols] += take(BLOCK, COARSE)
            rows = pl.ds(OUT_L2, BLOCK)
            grad[which, rows, cols] += take(BLOCK + COARSE, BLOCK)

        @pl.when(d_prev)
        def _():
            for which in range(2):
                z_out[which, pl.ds(0, RET), cols] = folded(which, cols)
                second = grad[which, pl.ds(OUT_L2 + HALF, HALF), cols]
                z_out[which, pl.ds(RET, HALF), cols] = second.astype(jnp.bfloat16)
            z_main(g).start()
            z_grad2(g).start()

        @pl.when(is_p)
        def _():
            for which in range(2):
                s_out[which, :, cols] = grad[which, pl.ds(OUT_L2 + HALF, HALF), cols].astype(jnp.bfloat16)
            sib_grad2(g).start()

    def send_peer(g):
        cols = pl.ds(g * width, width)

        @pl.when(p_next)
        def _():
            z_grad2(g).wait_recv()
            for which in range(2):
                grad[which, pl.ds(OUT_L2, HALF), cols] += (
                    z_in[which, pl.ds(RET, HALF), cols].astype(jnp.float32))

        @pl.when(is_p)
        def _():
            for which in range(2):
                ret_out[which, :, cols] = folded(which, cols)

        @pl.when(d_next)
        def _():
            z_main(g).wait_recv()

        @pl.when(is_d)
        def _():
            sib_grad2(g).wait_recv()
            for which in range(2):
                total = nn(coarse_matrix(), s_in[which, :, cols])
                total += z_in[which, pl.ds(0, RET), cols].astype(jnp.float32)
                ret_out[which, :, cols] = total.astype(jnp.bfloat16)
        ret(g).start()

    def finish(g):
        cols = pl.ds(g * width, width)
        ret(g).wait_recv()
        for which, ref in enumerate((gk_ref, gv_ref)):
            rows = pl.ds(outer_start, BLOCK)
            grad[which, rows, cols] += ret_in[which, pl.ds(0, BLOCK), cols].astype(jnp.float32)
            rows = pl.ds(OWN_L1 + inner_half, HALF)
            grad[which, rows, cols] += ret_in[which, pl.ds(BLOCK, HALF), cols].astype(jnp.float32)
            fine = grad[which, pl.ds(0, 2 * BLOCK), cols]
            fine += spread(own_matrix(), grad[which, pl.ds(OWN_L1, COARSE), cols])
            ref[:, cols] = fine.astype(jnp.bfloat16)

    heads = width // HEAD_DIM
    forward(0)
    for g in range(CHUNKS):
        if g + 1 < CHUNKS:
            forward(g + 1)
        share_far(g)
        sib_coarse(g).wait_recv()
        sib_fine(g).wait_recv()
        far(g).wait_recv()
        lax.fori_loop(g * heads, (g + 1) * heads, lambda h, c: (attend(h), c)[1], 0, unroll=2)
        back(g).start()
        if g > 0:
            send_outer(g - 1)
        if g > 1:
            send_peer(g - 2)
        if g >= LAG:
            finish(g - LAG)
    send_outer(CHUNKS - 1)
    for g in range(max(0, CHUNKS - 2), CHUNKS):
        send_peer(g)
    for g in range(max(0, CHUNKS - LAG), CHUNKS):
        finish(g)
    for g in range(CHUNKS):
        for item in (sib_fine, sib_coarse, p_fine, p_l1, far, back, ret):
            item(g).wait_send()

        @pl.when(is_p)
        def _():
            sib_grad2(g).wait_send()

        @pl.when(is_d)
        def _():
            sib_l2(g).wait_send()

        @pl.when(p_next)
        def _():
            z_l2(g).wait_send()

        @pl.when(d_next)
        def _():
            z_fine(g).wait_send()
            z_l1(g).wait_send()

        @pl.when(d_prev)
        def _():
            z_main(g).wait_send()
            z_grad2(g).wait_send()


def place(*refs):
    sems = refs[-1]
    copies = [pltpu.make_async_copy(refs[i], refs[4 + i], sems.at[i]) for i in range(4)]
    for item in copies:
        item.start()
    for item in copies:
        item.wait()


def body(queries, key_input, value_input, cotangent):
    rows, feat = queries.shape
    out = jax.ShapeDtypeStruct((rows, feat), jnp.bfloat16)
    results = pl.pallas_call(
        kernel,
        name="hier_attention",
        out_shape=[out] * 4,
        in_specs=[pl.BlockSpec(memory_space=pltpu.VMEM)] * 4,
        out_specs=[pl.BlockSpec(memory_space=pltpu.VMEM)] * 4,
        scratch_shapes=[
            pltpu.VMEM((2, CAND, feat), jnp.bfloat16),
            pltpu.VMEM((2, CAND, feat), jnp.float32),
            pltpu.VMEM((CAND, rows), jnp.float32),
            pltpu.VMEM((2, RELAY, feat), jnp.bfloat16),
            pltpu.VMEM((2, BACK, feat), jnp.bfloat16),
            pltpu.VMEM((2, BACK, feat), jnp.bfloat16),
            pltpu.VMEM((2, RET + HALF, feat), jnp.bfloat16),
            pltpu.VMEM((2, RET + HALF, feat), jnp.bfloat16),
            pltpu.VMEM((2, HALF, feat), jnp.bfloat16),
            pltpu.VMEM((2, HALF, feat), jnp.bfloat16),
            pltpu.VMEM((2, RET, feat), jnp.bfloat16),
            pltpu.VMEM((2, RET, feat), jnp.bfloat16),
            pltpu.SemaphoreType.DMA((STAGES, CHUNKS)),
            pltpu.SemaphoreType.DMA((STAGES, CHUNKS)),
        ],
        compiler_params=pltpu.CompilerParams(
            collective_id=0, has_side_effects=True, vmem_limit_bytes=56 * 1024 * 1024),
    )(queries, key_input, value_input, cotangent)
    return tuple(pl.pallas_call(
        place,
        name="place",
        out_shape=[out] * 4,
        in_specs=[pl.BlockSpec(memory_space=pltpu.VMEM)] * 4,
        out_specs=[pl.BlockSpec(memory_space=pl.ANY)] * 4,
        scratch_shapes=[pltpu.SemaphoreType.DMA((4,))],
    )(*results))


def solution(mesh):
    spec = P(("groups", "seq"), None)
    return jax.shard_map(
        body, mesh=mesh, in_specs=(spec,) * 4, out_specs=(spec,) * 4, check_vma=False)
```

```python
import math

import jax
import jax.numpy as jnp
from jax import lax
from jax.experimental import pallas as pl
from jax.experimental.pallas import tpu as pltpu
from jax.sharding import PartitionSpec as P

HEADS = 16
HEAD_DIM = 128
BLOCK = 64
HALF = BLOCK // 2
CHUNKS = 8
EARLY = 2
LAG = 8

SIB_FINE = 2 * BLOCK
OUT_FINE = SIB_FINE + BLOCK
OWN_L1 = OUT_FINE + BLOCK
OWN_L2 = OWN_L1 + BLOCK
SIB_L1 = OWN_L2 + HALF
SIB_L2 = SIB_L1 + BLOCK
OUT_L1 = SIB_L2 + HALF
OUT_L2 = OUT_L1 + BLOCK
FAR_L2 = OUT_L2 + BLOCK
CAND = FAR_L2 + BLOCK
COARSE = BLOCK + HALF
BACK = BLOCK + COARSE + BLOCK
RET = BLOCK + HALF
RELAY_L1 = BLOCK
RELAY_L2 = 2 * BLOCK
RELAY = RELAY_L2 + HALF
STAGES = 14

masked_score = -1e30
MESH = pl.DeviceIdType.MESH


def nt(a, b):
    return lax.dot_general(a, b, (((1,), (1,)), ((), ())), preferred_element_type=jnp.float32)


def nn(a, b):
    return lax.dot_general(a, b, (((1,), (0,)), ((), ())), preferred_element_type=jnp.float32)


def tn(a, b):
    return lax.dot_general(a, b, (((0,), (0,)), ((), ())), preferred_element_type=jnp.float32)


def pool_matrix(rows):
    row = lax.broadcasted_iota(jnp.int32, (rows // 2, rows), 0)
    col = lax.broadcasted_iota(jnp.int32, (rows // 2, rows), 1)
    return jnp.where((col >> 1) == row, 0.5, 0.0).astype(jnp.bfloat16)


def pooled(rows):
    return nn(pool_matrix(rows.shape[0]), rows).astype(jnp.bfloat16)


def spread_matrix(shape, row0, col0, rows, shift):
    row = lax.broadcasted_iota(jnp.int32, shape, 0) - row0
    col = lax.broadcasted_iota(jnp.int32, shape, 1) - col0
    hit = (row >= 0) & (row < rows) & ((row >> shift) == col)
    return jnp.where(hit, 0.5 ** shift, 0.0)


def spread(matrix, grads):
    matrix = matrix.astype(jnp.bfloat16)
    high = grads.astype(jnp.bfloat16)
    low = (grads - high.astype(jnp.float32)).astype(jnp.bfloat16)
    return nn(jnp.concatenate([matrix, matrix], axis=1), jnp.concatenate([high, low], axis=0))


def message_matrix():
    shape = (RET, BLOCK)
    return (spread_matrix(shape, 0, 0, BLOCK, 1)
            + spread_matrix(shape, 0, HALF, BLOCK, 2)
            + spread_matrix(shape, BLOCK, HALF + HALF // 2, HALF, 1))


def coarse_matrix():
    shape = (RET, HALF)
    return (spread_matrix(shape, 0, 0, BLOCK, 2)
            + spread_matrix(shape, BLOCK, HALF // 2, HALF, 1)).astype(jnp.bfloat16)


def own_matrix():
    shape = (2 * BLOCK, COARSE)
    return (spread_matrix(shape, 0, 0, 2 * BLOCK, 1)
            + spread_matrix(shape, 0, BLOCK, 2 * BLOCK, 2))


def kernel(q_ref, k_ref, v_ref, do_ref, att_ref, gq_ref, gk_ref, gv_ref,
           kv, grad, bias, relay, back_out, back_in, z_out, z_in, s_out, s_in,
           ret_out, ret_in, send_sem, recv_sem):
    count = lax.axis_size("seq")
    me = lax.axis_index("seq")
    side = lax.rem(me, 2)
    chip = me // 2
    odd = lax.rem(chip, 2)
    sib = me + 1 - 2 * side
    is_p = lax.rem(side + chip, 2) == 1
    is_d = jnp.logical_not(is_p)
    peer = 2 * (chip + 1 - 2 * odd) + 1 - side
    step = 4 - 8 * odd
    has_next = (me + step >= 0) & (me + step < count)
    has_prev = (me - step >= 0) & (me - step < count)
    has_outer = is_p | has_prev
    has_far = is_d | has_prev
    d_next = is_d & has_next
    d_prev = is_d & has_prev
    p_next = is_p & has_next
    feat = q_ref.shape[1]
    width = feat // CHUNKS
    scale = HEAD_DIM ** -0.5
    inner_start = pl.multiple_of(BLOCK * (1 - side), BLOCK)
    outer_start = pl.multiple_of(BLOCK * side, BLOCK)
    inner_half = pl.multiple_of(HALF * (1 - side), HALF)

    barrier = pltpu.get_barrier_semaphore()

    def greet(target):
        pl.semaphore_signal(barrier, inc=1, device_id={"seq": target}, device_id_type=MESH)

    greet(sib)
    greet(peer)

    @pl.when(d_next)
    def _():
        greet(me + step)

    @pl.when(p_next)
    def _():
        greet(sib + step)

    @pl.when(d_prev)
    def _():
        greet(me - step)
        greet(sib - step)

    own = pl.ds(0, 2 * BLOCK)
    for which, ref in enumerate((k_ref, v_ref)):
        kv[which, own, :] = ref[...]

    @pl.when(jnp.logical_not(has_outer))
    def _():
        for which in range(2):
            kv[which, OUT_FINE:OUT_FINE + BLOCK, :] = jnp.zeros((BLOCK, feat), jnp.bfloat16)
            kv[which, OUT_L1:OUT_L1 + 2 * BLOCK, :] = jnp.zeros((2 * BLOCK, feat), jnp.bfloat16)

    @pl.when(is_d & jnp.logical_not(has_next))
    def _():
        z_in[:, 0:RET, :] = jnp.zeros((2, RET, feat), jnp.bfloat16)

    lane = lax.broadcasted_iota(jnp.int32, (BLOCK, 2 * BLOCK), 1)
    is_outer_lane = (lane >> 6) == side
    zero = jnp.zeros((BLOCK, 2 * BLOCK), jnp.float32)
    bias[0:BLOCK] = zero
    bias[BLOCK:2 * BLOCK] = zero
    bias[SIB_FINE:SIB_FINE + BLOCK] = jnp.where(is_outer_lane, masked_score, zero)
    bias[OUT_FINE:OUT_FINE + BLOCK] = jnp.where(is_outer_lane & has_outer, zero, masked_score)
    bias[OWN_L1:OWN_L1 + BLOCK] = zero + 1.0
    bias[OWN_L2:OWN_L2 + HALF] = zero[:HALF] + 2.0
    bias[SIB_L1:SIB_L1 + BLOCK] = zero + 1.0
    bias[SIB_L2:SIB_L2 + HALF] = zero[:HALF] + 2.0
    bias[OUT_L1:OUT_L1 + BLOCK] = jnp.where(has_outer, zero + 1.0, masked_score)
    bias[OUT_L2:OUT_L2 + BLOCK] = jnp.where(has_outer, zero + 2.0, masked_score)
    bias[FAR_L2:FAR_L2 + BLOCK] = jnp.where(has_far, zero + 2.0, masked_score)

    peers = 2 + has_next.astype(jnp.int32) + 2 * d_prev.astype(jnp.int32)
    pl.semaphore_wait(barrier, peers)

    def copy(stage, chunk, src, src_row, dst, dst_row, rows, target):
        cols = pl.ds(chunk * width, width)
        return pltpu.make_async_remote_copy(
            src_ref=src.at[:, pl.ds(src_row, rows), cols],
            dst_ref=dst.at[:, pl.ds(dst_row, rows), cols],
            send_sem=send_sem.at[stage, chunk],
            recv_sem=recv_sem.at[stage, chunk],
            device_id={"seq": target},
            device_id_type=MESH,
        )

    def sib_fine(g):
        return copy(0, g, kv, inner_start, kv, SIB_FINE, BLOCK, sib)

    def sib_coarse(g):
        return copy(1, g, kv, OWN_L1, kv, SIB_L1, COARSE, sib)

    def p_fine(g):
        return copy(2, g, kv, outer_start, kv, OUT_FINE, BLOCK, peer)

    def p_l1(g):
        return copy(3, g, kv, OWN_L1 + inner_half, kv, OUT_L1 + HALF, HALF, peer)

    def d_fine(g):
        return copy(2, g, kv, outer_start, relay, 0, BLOCK, peer)

    def d_l1(g):
        return copy(3, g, kv, OWN_L1 + inner_half, relay, RELAY_L1 + HALF, HALF, peer)

    def z_fine(g):
        return copy(4, g, relay, 0, kv, OUT_FINE, BLOCK, me + step)

    def z_l1(g):
        return copy(5, g, relay, RELAY_L1 + HALF, kv, OUT_L1 + HALF, HALF, me + step)

    def z_l2(g):
        return copy(6, g, kv, OUT_L2, kv, OUT_L2 + HALF, HALF, sib + step)

    def sib_l2(g):
        return copy(7, g, relay, RELAY_L2, kv, OUT_L2 + HALF, HALF, sib)

    def far(g):
        return copy(8, g, kv, OUT_L2, kv, FAR_L2, BLOCK, sib)

    def back(g):
        return copy(9, g, back_out, 0, back_in, 0, BACK, sib)

    def z_main(g):
        return copy(10, g, z_out, 0, z_in, 0, RET, me - step)

    def z_grad2(g):
        return copy(11, g, z_out, RET, z_in, RET, HALF, sib - step)

    def sib_grad2(g):
        return copy(12, g, s_out, 0, s_in, 0, HALF, sib)

    def ret(g):
        return copy(13, g, ret_out, 0, ret_in, 0, RET, peer)

    def start_fine(g):
        @pl.when(is_p)
        def _():
            p_fine(g).start()

        @pl.when(is_d)
        def _():
            d_fine(g).start()

    def start_l1(g):
        @pl.when(is_p)
        def _():
            p_l1(g).start()

        @pl.when(is_d)
        def _():
            d_l1(g).start()

    for g in range(EARLY):
        start_fine(g)
    for which in range(2):
        first = pooled(kv[which, own, :])
        kv[which, OWN_L1:OWN_L1 + BLOCK, :] = first
        kv[which, OWN_L2:OWN_L2 + HALF, :] = pooled(first)
    for g in range(CHUNKS):
        if g >= EARLY:
            start_fine(g)
        start_l1(g)
        sib_coarse(g).start()
        sib_fine(g).start()

    def derive(ref, which, cols, fine, first, second):
        ref[which, pl.ds(first, HALF), cols] = pooled(ref[which, pl.ds(fine, BLOCK), cols])
        ref[which, pl.ds(second, HALF), cols] = pooled(ref[which, pl.ds(first, BLOCK), cols])

    def forward(g):
        cols = pl.ds(g * width, width)

        @pl.when(is_p)
        def _():
            p_fine(g).wait_recv()
            p_l1(g).wait_recv()
            for which in range(2):
                derive(kv, which, cols, OUT_FINE, OUT_L1, OUT_L2)

        @pl.when(p_next)
        def _():
            z_l2(g).start()

        @pl.when(is_d)
        def _():
            d_fine(g).wait_recv()
            d_l1(g).wait_recv()

        @pl.when(d_next)
        def _():
            z_fine(g).start()
            z_l1(g).start()

        @pl.when(is_d)
        def _():
            for which in range(2):
                derive(relay, which, cols, 0, RELAY_L1, RELAY_L2)
            sib_l2(g).start()

    def share_far(g):
        cols = pl.ds(g * width, width)

        @pl.when(is_p)
        def _():
            sib_l2(g).wait_recv()

        @pl.when(d_prev)
        def _():
            z_fine(g).wait_recv()
            z_l1(g).wait_recv()
            for which in range(2):
                derive(kv, which, cols, OUT_FINE, OUT_L1, OUT_L2)
            z_l2(g).wait_recv()
        far(g).start()

    def attend(h):
        cols = pl.ds(pl.multiple_of(h * HEAD_DIM, HEAD_DIM), HEAD_DIM)
        q = q_ref[:, cols]
        do = do_ref[:, cols]
        k = kv[0, :, cols]
        v = kv[1, :, cols]
        scores = nt(k, q) * (scale * math.log2(math.e)) + bias[...]
        largest = jnp.max(scores, axis=0, keepdims=True)
        raised = jnp.exp2(scores - largest)
        weights = raised * (1.0 / jnp.sum(raised, axis=0, keepdims=True))
        weights_b = weights.astype(jnp.bfloat16)
        attended = tn(weights_b, v).astype(jnp.bfloat16)
        att_ref[:, cols] = attended
        product = do.astype(jnp.float32) * attended.astype(jnp.float32)
        row_dots = jnp.sum(product.T, axis=0, keepdims=True)
        grad_scores = (weights * (nt(v, do) - row_dots) * scale).astype(jnp.bfloat16)
        gq_ref[:, cols] = tn(grad_scores, k).astype(jnp.bfloat16)
        for which, part in ((0, nn(grad_scores, q)), (1, nn(weights_b, do))):
            for start, end in ((0, SIB_FINE), (OUT_FINE, SIB_L1), (OUT_L1, FAR_L2)):
                grad[which, start:end, cols] = part[start:end]
            for dst, src, rows in ((0, SIB_FINE, BLOCK), (BLOCK, SIB_L1, COARSE),
                                   (BLOCK + COARSE, FAR_L2, BLOCK)):
                back_out[which, dst:dst + rows, cols] = part[src:src + rows].astype(jnp.bfloat16)

    def folded(which, cols):
        coarse = jnp.concatenate([grad[which, pl.ds(OUT_L1, HALF), cols],
                                  grad[which, pl.ds(OUT_L2, HALF), cols]], axis=0)
        total = spread(message_matrix(), coarse)
        total += jnp.concatenate([grad[which, pl.ds(OUT_FINE, BLOCK), cols],
                                  grad[which, pl.ds(OUT_L1 + HALF, HALF), cols]], axis=0)
        return total.astype(jnp.bfloat16)

    def send_outer(g):
        cols = pl.ds(g * width, width)
        back(g).wait_recv()
        for which in range(2):
            def take(row, rows):
                return back_in[which, pl.ds(row, rows), cols].astype(jnp.float32)
            rows = pl.ds(inner_start, BLOCK)
            grad[which, rows, cols] += take(0, BLOCK)
            rows = pl.ds(OWN_L1, COARSE)
            grad[which, rows, cols] += take(BLOCK, COARSE)
            rows = pl.ds(OUT_L2, BLOCK)
            grad[which, rows, cols] += take(BLOCK + COARSE, BLOCK)

        @pl.when(d_prev)
        def _():
            for which in range(2):
                z_out[which, pl.ds(0, RET), cols] = folded(which, cols)
                second = grad[which, pl.ds(OUT_L2 + HALF, HALF), cols]
                z_out[which, pl.ds(RET, HALF), cols] = second.astype(jnp.bfloat16)
            z_main(g).start()
            z_grad2(g).start()

        @pl.when(is_p)
        def _():
            for which in range(2):
                s_out[which, :, cols] = grad[which, pl.ds(OUT_L2 + HALF, HALF), cols].astype(jnp.bfloat16)
            sib_grad2(g).start()

    def send_peer(g):
        cols = pl.ds(g * width, width)

        @pl.when(p_next)
        def _():
            z_grad2(g).wait_recv()
            for which in range(2):
                grad[which, pl.ds(OUT_L2, HALF), cols] += (
                    z_in[which, pl.ds(RET, HALF), cols].astype(jnp.float32))

        @pl.when(is_p)
        def _():
            for which in range(2):
                ret_out[which, :, cols] = folded(which, cols)

        @pl.when(d_next)
        def _():
            z_main(g).wait_recv()

        @pl.when(is_d)
        def _():
            sib_grad2(g).wait_recv()
            for which in range(2):
                total = nn(coarse_matrix(), s_in[which, :, cols])
                total += z_in[which, pl.ds(0, RET), cols].astype(jnp.float32)
                ret_out[which, :, cols] = total.astype(jnp.bfloat16)
        ret(g).start()

    def finish(g):
        cols = pl.ds(g * width, width)
        ret(g).wait_recv()
        for which, ref in enumerate((gk_ref, gv_ref)):
            rows = pl.ds(outer_start, BLOCK)
            grad[which, rows, cols] += ret_in[which, pl.ds(0, BLOCK), cols].astype(jnp.float32)
            rows = pl.ds(OWN_L1 + inner_half, HALF)
            grad[which, rows, cols] += ret_in[which, pl.ds(BLOCK, HALF), cols].astype(jnp.float32)
            fine = grad[which, pl.ds(0, 2 * BLOCK), cols]
            fine += spread(own_matrix(), grad[which, pl.ds(OWN_L1, COARSE), cols])
            ref[:, cols] = fine.astype(jnp.bfloat16)

    heads = width // HEAD_DIM
    forward(0)
    for g in range(CHUNKS):
        if g + 1 < CHUNKS:
            forward(g + 1)
        share_far(g)
        sib_coarse(g).wait_recv()
        sib_fine(g).wait_recv()
        far(g).wait_recv()
        lax.fori_loop(g * heads, (g + 1) * heads, lambda h, c: (attend(h), c)[1], 0, unroll=2)
        back(g).start()
        if g > 0:
            send_outer(g - 1)
        if g > 1:
            send_peer(g - 2)
        if g >= LAG:
            finish(g - LAG)
    send_outer(CHUNKS - 1)
    for g in range(max(0, CHUNKS - 2), CHUNKS):
        send_peer(g)
    for g in range(max(0, CHUNKS - LAG), CHUNKS):
        finish(g)
    for g in range(CHUNKS):
        for item in (sib_fine, sib_coarse, p_fine, p_l1, far, back, ret):
            item(g).wait_send()

        @pl.when(is_p)
        def _():
            sib_grad2(g).wait_send()

        @pl.when(is_d)
        def _():
            sib_l2(g).wait_send()

        @pl.when(p_next)
        def _():
            z_l2(g).wait_send()

        @pl.when(d_next)
        def _():
            z_fine(g).wait_send()
            z_l1(g).wait_send()

        @pl.when(d_prev)
        def _():
            z_main(g).wait_send()
            z_grad2(g).wait_send()


def place(*refs):
    held, sems = refs[8:]
    loads = [pltpu.make_async_copy(refs[i], held.at[i], sems.at[0, i]) for i in range(4)]
    stores = [pltpu.make_async_copy(held.at[i], refs[4 + i], sems.at[1, i]) for i in range(4)]
    for item in loads:
        item.start()
    for load, store in zip(loads, stores):
        load.wait()
        store.start()
    for item in stores:
        item.wait()


def body(queries, key_input, value_input, cotangent):
    rows, feat = queries.shape
    out = jax.ShapeDtypeStruct((rows, feat), jnp.bfloat16)
    results = pl.pallas_call(
        kernel,
        name="hier_attention",
        out_shape=[out] * 4,
        in_specs=[pl.BlockSpec(memory_space=pltpu.VMEM)] * 4,
        out_specs=[pl.BlockSpec(memory_space=pltpu.VMEM)] * 4,
        scratch_shapes=[
            pltpu.VMEM((2, CAND, feat), jnp.bfloat16),
            pltpu.VMEM((2, CAND, feat), jnp.float32),
            pltpu.VMEM((CAND, rows), jnp.float32),
            pltpu.VMEM((2, RELAY, feat), jnp.bfloat16),
            pltpu.VMEM((2, BACK, feat), jnp.bfloat16),
            pltpu.VMEM((2, BACK, feat), jnp.bfloat16),
            pltpu.VMEM((2, RET + HALF, feat), jnp.bfloat16),
            pltpu.VMEM((2, RET + HALF, feat), jnp.bfloat16),
            pltpu.VMEM((2, HALF, feat), jnp.bfloat16),
            pltpu.VMEM((2, HALF, feat), jnp.bfloat16),
            pltpu.VMEM((2, RET, feat), jnp.bfloat16),
            pltpu.VMEM((2, RET, feat), jnp.bfloat16),
            pltpu.SemaphoreType.DMA((STAGES, CHUNKS)),
            pltpu.SemaphoreType.DMA((STAGES, CHUNKS)),
        ],
        compiler_params=pltpu.CompilerParams(
            collective_id=0, has_side_effects=True, vmem_limit_bytes=56 * 1024 * 1024),
    )(queries, key_input, value_input, cotangent)
    return tuple(pl.pallas_call(
        place,
        name="place",
        out_shape=[out] * 4,
        in_specs=[pl.BlockSpec(memory_space=pl.ANY)] * 4,
        out_specs=[pl.BlockSpec(memory_space=pl.ANY)] * 4,
        scratch_shapes=[pltpu.VMEM((4, rows, feat), jnp.bfloat16), pltpu.SemaphoreType.DMA((2, 4))],
    )(*results))


def solution(mesh):
    spec = P(("groups", "seq"), None)
    return jax.shard_map(
        body, mesh=mesh, in_specs=(spec,) * 4, out_specs=(spec,) * 4, check_vma=False)
```
